32 devices in a mesh: dp: 8 (over y, x, core), mp: 4 (over z).
Axes of the slice: x: 2, y: 2, z: 4, core: 2. Of those that a mesh axis runs over, the one named last changes fastest.
Arguments:
- ref_hidden: bfloat16 [512, 2048], P('dp', 'mp'), may hold values from -80 to 80
- proxy_hidden: bfloat16 [512, 2048], P('dp', 'mp'), may hold values from -80 to 80
- ref_gain: float32 [2048], replicated, may hold values from 0.5 to 1.5
- proxy_gain: float32 [2048], replicated, may hold values from 0.5 to 1.5
- ref_head: bfloat16 [2048, 128256], P(None, ('dp', 'mp')), may hold values from -16 to 16
- proxy_head: bfloat16 [2048, 128256], P(None, ('dp', 'mp')), may hold values from -16 to 16
- token_ids: int32 [512], P('dp'), may hold values from 0 to 128255
- bucket_ids: int32 [512], P(('dp', 'mp')), may hold values from 0 to 4095
- domain_of_bucket: int32 [4096], replicated, may hold values from 0 to 21
- prior_weights: float32 [22], replicated, may hold values from 0.01 to 0.1
Outputs:
- ref_loss: float32 [512], P(('dp', 'mp'))
- proxy_loss: float32 [512], P(('dp', 'mp'))
- bucket_excess: float32 [4096], P(('dp', 'mp'))
- domain_log_weights: float32 [22], replicated
The draws below stay inside these ranges and needn't reach their ends.
All inputs are finite; a program needn't handle non-finite values.
Results may differ from the reference program's by a relative error of at most 0.0035.
Values may be sent and summed in bfloat16 or wider, within the bound.
No kernel may reach another device: no remote copies, remote signals or barrier semaphores. Data moves between devices by JAX's collectives and lax.ppermute only.
A program may use at most 128 MiB of HBM per device.

```python
import math
import jax
import jax.numpy as jnp
import numpy as np
from jax import lax

D = 2048
VOCAB = 128256
BUCKETS = 4096
DOMAINS = 22
TOKENS = 512


def head_draw(key, which):
    weights = jax.random.normal(jax.random.fold_in(key, 11 + which), (D, VOCAB), jnp.float32) * (3.0 / math.sqrt(D))
    return weights.astype(jnp.bfloat16)


def hidden_draw(key, which):
    noise = jax.random.normal(jax.random.fold_in(key, 21 + which), (TOKENS, D), jnp.float32)
    scales = jnp.exp(jax.random.uniform(jax.random.fold_in(key, 31 + which), (TOKENS, 1), jnp.float32, 0.0, math.log(10.0)))
    values = noise
    return (values * scales).astype(jnp.bfloat16)


def draw_ref_hidden(key, part):
    return hidden_draw(key, 0)


def draw_proxy_hidden(key, part):
    return hidden_draw(key, 1)


def draw_ref_head(key, part):
    return head_draw(key, 0)


def draw_proxy_head(key, part):
    return head_draw(key, 1)


def set_ends(result, own_key, smallest, top_value):
    shape = result.shape
    place = [jax.random.randint(jax.random.fold_in(own_key, axis), (), 0, shape[axis]) for axis in range(len(shape))]
    result = result.at[tuple(place)].set(smallest)
    longest = shape.index(max(shape))
    place[longest] = (place[longest] + 1) % shape[longest]
    return result.at[tuple(place)].set(top_value)


def skewed_wide(own_key, shape, count, lean):
    loads = [min(1 << octave, count + 1 - (1 << octave)) * (1 << 20) // math.isqrt((1 << octave) ** lean) + 1 for octave in range((count + 1).bit_length()) if 1 << octave <= count]
    scale = 1 + sum(loads) // (1 << 30)
    grid = np.cumsum(np.array([max(1, weight // scale) for weight in loads]))
    pick = jax.random.randint(jax.random.fold_in(own_key, 1), shape, 0, int(grid[len(loads) - 1]))
    start = jnp.left_shift(1, jnp.searchsorted(jnp.asarray(grid, jnp.int32), pick, side="right").astype(jnp.int32))
    grade = start - 1 + jax.random.randint(jax.random.fold_in(own_key, 4), shape, 0, 1 << 30) % jnp.minimum(start, count + 1 - start)
    return jax.random.permutation(jax.random.fold_in(own_key, 2), count)[grade].astype(jnp.int32)


def setup_inputs(seed: int = 0) -> dict:
    key_list = jax.random.split(jax.random.key(seed), 11)
    ref_hidden = draw_ref_hidden(jax.random.fold_in(key_list[10], 71), 0)
    proxy_hidden = draw_proxy_hidden(jax.random.fold_in(key_list[10], 71), 0)
    ref_gain = jnp.clip(1.0 + 0.1 * jax.random.normal(key_list[2], (D,), jnp.float32), 0.5, 1.5)
    proxy_gain = jnp.clip(1.0 + 0.1 * jax.random.normal(key_list[3], (D,), jnp.float32), 0.5, 1.5)
    ref_head = draw_ref_head(jax.random.fold_in(key_list[10], 71), 0)
    proxy_head = draw_proxy_head(jax.random.fold_in(key_list[10], 71), 0)
    token_ids = set_ends(skewed_wide(key_list[6], (TOKENS,), VOCAB, 2), jax.random.fold_in(key_list[6], 3), 0, VOCAB - 1).astype(jnp.int32)
    bucket_ids = set_ends(jax.random.randint(key_list[7], (TOKENS,), 0, BUCKETS), jax.random.fold_in(key_list[7], 1), 0, BUCKETS - 1).astype(jnp.int32)
    domain_of_bucket = set_ends(jax.random.randint(key_list[8], (BUCKETS,), 0, DOMAINS), jax.random.fold_in(key_list[8], 1), 0, DOMAINS - 1).astype(jnp.int32)
    prior_weights = jnp.clip(jnp.exp(jax.random.uniform(key_list[9], (DOMAINS,), jnp.float32, math.log(0.01), math.log(0.1))), 0.01, 0.1)
    return {"ref_hidden": ref_hidden, "proxy_hidden": proxy_hidden, "ref_gain": ref_gain, "proxy_gain": proxy_gain, "ref_head": ref_head, "proxy_head": proxy_head, "token_ids": token_ids, "bucket_ids": bucket_ids, "domain_of_bucket": domain_of_bucket, "prior_weights": prior_weights}


def normalize(hidden, gain):
    values = hidden.astype(jnp.float32)
    scale = lax.rsqrt(lax.optimization_barrier(jnp.mean(values * values, -1, keepdims=True)) + 1e-05)
    return (values * scale * gain).astype(jnp.bfloat16)

def score(hidden, gain, head, token_ids):
    normed = normalize(hidden, gain)
    width = VOCAB // 32
    rows = normed.shape[0]

    def block_step(index, carry):
        top, total = carry
        piece = lax.dynamic_slice_in_dim(head, index * width, width, 1)
        logits = jnp.dot(normed, piece, preferred_element_type=jnp.float32)
        newtop = jnp.maximum(top, lax.optimization_barrier(jnp.max(logits, -1)))
        total = total * jnp.exp(top - newtop) + lax.optimization_barrier(jnp.sum(jnp.exp(logits - newtop[:, None]), -1))
        return (newtop, total)
    start = (jnp.full((rows,), -jnp.inf, jnp.float32), jnp.zeros((rows,), jnp.float32))
    top, total = lax.fori_loop(0, 32, block_step, start)
    columns = jnp.take(head, token_ids, axis=1)
    target = lax.optimization_barrier(jnp.sum(normed.astype(jnp.float32) * columns.T.astype(jnp.float32), -1))
    return top + jnp.log(total) - target

def reference(ref_hidden, proxy_hidden, ref_gain, proxy_gain, ref_head, proxy_head, token_ids, bucket_ids, domain_of_bucket, prior_weights):
    ref_loss = score(ref_hidden, ref_gain, ref_head, token_ids)
    proxy_loss = score(proxy_hidden, proxy_gain, proxy_head, token_ids)
    excess = jnp.maximum(proxy_loss - ref_loss, 0.0)
    bucket_sum = jax.ops.segment_sum(excess, bucket_ids, BUCKETS)
    bucket_count = jax.ops.segment_sum(jnp.ones_like(excess), bucket_ids, BUCKETS)
    bucket_excess = bucket_sum / jnp.maximum(bucket_count, 1.0)
    domain_sum = jax.ops.segment_sum(bucket_sum, domain_of_bucket, DOMAINS)
    domain_count = jax.ops.segment_sum(bucket_count, domain_of_bucket, DOMAINS)
    domain_excess = domain_sum / jnp.maximum(domain_count, 1.0)
    weights = jax.nn.softmax(jnp.log(prior_weights) + 1.0 * domain_excess)
    domain_log_weights = jnp.log(0.999 * weights + 0.001 / DOMAINS)
    return (ref_loss, proxy_loss, bucket_excess, domain_log_weights)
```

```python
import functools

import jax
import jax.numpy as jnp
from jax import lax
from jax.experimental import pallas as pl
from jax.experimental.pallas import tpu as pltpu
from jax.sharding import PartitionSpec as P

AXES = ("dp", "mp")
LOW = -1e30


def swap(x, dp, mp, flip_dp, flip_mp):
    pairs = [
        (d * mp + m, (d ^ flip_dp) * mp + (m ^ flip_mp)) for d in range(dp) for m in range(mp)
    ]
    return lax.ppermute(x, AXES, pairs)


def gather(hidden, dp, mp):
    slices = jnp.stack([hidden] + [swap(hidden, dp, mp, 0, k) for k in range(1, mp)])
    chips = jnp.stack([slices] + [swap(slices, dp, mp, 2 * k, 0) for k in range(1, dp // 2)])
    return chips, swap(chips, dp, mp, 1, 0)


def stats_kernel(
    bounds, vocab, where_ref, ids_ref, gain_ref, mine_ref, theirs_ref, head_ref, out_ref,
    words, states, sems,
):
    tokens, width = states.shape
    chips, slices, rows, depth = mine_ref.shape
    copies = [
        pltpu.make_async_copy(
            head_ref.at[pl.ds(start, size)], words.at[pl.ds(start, size)], sems.at[n]
        )
        for n, (start, size) in enumerate(bounds)
    ]
    for copy in copies:
        copy.start()
    dp_at, mp_at, first = where_ref[0], where_ref[1], where_ref[2]
    for core, source in enumerate((mine_ref, theirs_ref)):

        def chip_step(chip, carry):
            block = (dp_at ^ core) ^ (2 * chip)
            place = pl.ds(pl.multiple_of(block * rows, rows), rows)
            total = jnp.zeros((rows, 1), jnp.float32)
            for piece in range(slices):
                values = source[chip, piece].astype(jnp.float32)
                total = total + jnp.sum(values * values, -1, keepdims=True)
            scale = lax.rsqrt(total / width + 1e-05)
            for piece in range(slices):
                lanes = pl.ds(pl.multiple_of((mp_at ^ piece) * depth, depth), depth)
                values = source[chip, piece].astype(jnp.float32)
                states[place, lanes] = (values * scale * gain_ref[:, lanes]).astype(jnp.bfloat16)
            return carry

        lax.fori_loop(0, chips, chip_step, 0)
    top = jnp.full((8, tokens), LOW, jnp.float32)
    total = jnp.zeros((8, tokens), jnp.float32)
    target = jnp.zeros((8, tokens), jnp.float32)
    wanted = ids_ref[...] - first
    for copy, (start, size) in zip(copies, bounds):
        copy.wait()
        logits = lax.dot_general(
            words[pl.ds(start, size), :],
            states[...],
            (((1,), (1,)), ((), ())),
            preferred_element_type=jnp.float32,
        )
        row = lax.broadcasted_iota(jnp.int32, (size, tokens), 0) + start
        if start + size > vocab:
            logits = jnp.where(row < vocab, logits, LOW)
        hit = jnp.where(row == wanted, logits, 0.0)
        logits = logits.reshape(size // 8, 8, tokens)
        fresh = jnp.maximum(top, jnp.max(logits, 0))
        total = total * jnp.exp(top - fresh) + jnp.sum(jnp.exp(logits - fresh[None]), 0)
        target = target + jnp.sum(hit.reshape(size // 8, 8, tokens), 0)
        top = fresh
    peak = jnp.max(top, 0, keepdims=True)
    out_ref[0:1, :] = peak + jnp.log(jnp.sum(total * jnp.exp(top - peak), 0, keepdims=True))
    out_ref[1:2, :] = jnp.sum(target, 0, keepdims=True)


def stats(where, ids, gain, mine, theirs, head):
    chips, slices, rows, depth = mine.shape
    tokens, width, vocab = 2 * chips * rows, slices * depth, head.shape[1]
    words = head.T
    if vocab % 8:
        words = jnp.pad(words, ((0, -vocab % 8), (0, 0)))
    height = words.shape[0]
    step = 512
    bounds = [(start, min(step, height - start)) for start in range(0, height, step)]
    vmem = pl.BlockSpec(memory_space=pltpu.VMEM)
    return pl.pallas_call(
        functools.partial(stats_kernel, bounds, vocab),
        in_specs=[pl.BlockSpec(memory_space=pltpu.SMEM)] + [vmem] * 4
        + [pl.BlockSpec(memory_space=pl.ANY)],
        out_specs=vmem,
        out_shape=jax.ShapeDtypeStruct((2, tokens), jnp.float32),
        scratch_shapes=[
            pltpu.VMEM((height, width), jnp.bfloat16),
            pltpu.VMEM((tokens, width), jnp.bfloat16),
            pltpu.SemaphoreType.DMA((len(bounds),)),
        ],
        compiler_params=pltpu.CompilerParams(vmem_limit_bytes=40 * 2**20),
        cost_estimate=pl.CostEstimate(
            flops=2 * tokens * width * vocab,
            bytes_accessed=2 * width * vocab,
            transcendentals=tokens * vocab,
        ),
        name="stats",
    )(where, ids, gain, mine, theirs, words)


def merge(left, right):
    peak = jnp.maximum(left, right)
    lse = peak + jnp.log(jnp.exp(left - peak) + jnp.exp(right - peak))
    row = lax.broadcasted_iota(jnp.int32, left.shape, 0)
    return jnp.where(row < 2, lse, left + right)


def finish_kernel(buckets, domains, where_ref, table_ref, prior_ref, loss_ref, bucket_ref, domain_ref):
    tokens = table_ref.shape[1]
    losses = table_ref[0:2, :] - table_ref[2:4, :]
    loss_ref[...] = losses
    excess = jnp.maximum(losses[1:2, :] - losses[0:1, :], 0.0)
    ids = table_ref[4:6, :].astype(jnp.int32)
    pad = domain_ref.shape[1]
    own = lax.broadcasted_iota(jnp.int32, (buckets, tokens), 0) + where_ref[3]
    every = lax.broadcasted_iota(jnp.int32, (pad, tokens), 0)
    terms = jnp.concatenate(
        [excess, jnp.ones_like(excess), jnp.zeros((6, tokens), jnp.float32)], 0
    )

    def sums(hot):
        return lax.dot_general(
            terms,
            hot.astype(jnp.float32),
            (((1,), (1,)), ((), ())),
            precision=lax.Precision.HIGHEST,
            preferred_element_type=jnp.float32,
        )

    table = sums(own == ids[0:1, :])
    bucket_ref[...] = table[0:1, :] / jnp.maximum(table[1:2, :], 1.0)
    table = sums(every == ids[1:2, :])
    score = jnp.log(prior_ref[...]) + table[0:1, :] / jnp.maximum(table[1:2, :], 1.0)
    real = lax.broadcasted_iota(jnp.int32, (1, pad), 1) < domains
    score = jnp.where(real, score, LOW)
    grown = jnp.exp(score - jnp.max(score, -1, keepdims=True))
    weights = grown / jnp.sum(grown, -1, keepdims=True)
    domain_ref[...] = jnp.log(0.999 * weights + 0.001 / domains)


def on_device(
    ref_hidden, proxy_hidden, ref_gain, proxy_gain, ref_head, proxy_head,
    token_ids, bucket_ids, domain_of_bucket, prior_weights,
):
    dp, mp = lax.axis_size("dp"), lax.axis_size("mp")
    dp_at, mp_at = lax.axis_index("dp"), lax.axis_index("mp")
    device = dp_at * mp + mp_at
    vocab_dev = ref_head.shape[1]
    own_rows = bucket_ids.shape[0]
    tokens = own_rows * dp * mp
    buckets, domains = domain_of_bucket.shape[0], prior_weights.shape[0]
    bucket_dev = buckets // (dp * mp)
    where = jnp.stack([dp_at, mp_at, device * vocab_dev, device * bucket_dev]).astype(jnp.int32)
    ids = lax.all_gather(token_ids, "dp", axis=0, tiled=True)[None]

    ref_mine, ref_theirs = gather(ref_hidden, dp, mp)
    proxy_mine, proxy_theirs = gather(proxy_hidden, dp, mp)
    first = stats(where, ids, ref_gain[None], ref_mine, ref_theirs, ref_head)
    second = stats(where, ids, proxy_gain[None], proxy_mine, proxy_theirs, proxy_head)

    hot = bucket_ids[:, None] == lax.broadcasted_iota(jnp.int32, (1, buckets), 1)
    own_domain = jnp.sum(jnp.where(hot, domain_of_bucket[None], 0), -1)
    labels = jnp.stack([bucket_ids, own_domain]).astype(jnp.float32)
    labels = lax.dynamic_update_slice(
        jnp.zeros((4, tokens), jnp.float32), labels, (0, device * own_rows)
    )
    table = jnp.concatenate(
        [first[0:1], second[0:1], first[1:2], second[1:2], labels], 0
    )
    flips = [(1 << n, 0) for n in range(dp.bit_length() - 1)]
    flips += [(0, 1 << n) for n in range(mp.bit_length() - 1)]
    for flip_dp, flip_mp in flips:
        table = merge(table, swap(table, dp, mp, flip_dp, flip_mp))

    pad = 128
    vmem = pl.BlockSpec(memory_space=pltpu.VMEM)
    losses, bucket_excess, domain_log_weights = pl.pallas_call(
        functools.partial(finish_kernel, bucket_dev, domains),
        in_specs=[pl.BlockSpec(memory_space=pltpu.SMEM), vmem, vmem],
        out_specs=[vmem] * 3,
        out_shape=[
            jax.ShapeDtypeStruct((2, tokens), jnp.float32),
            jax.ShapeDtypeStruct((1, bucket_dev), jnp.float32),
            jax.ShapeDtypeStruct((1, pad), jnp.float32),
        ],
        name="finish",
    )(where, table, jnp.pad(prior_weights, (0, pad - domains), constant_values=1.0)[None])
    own = lax.dynamic_slice_in_dim(losses, device * own_rows, own_rows, 1)
    return (own[0], own[1], bucket_excess[0], domain_log_weights[0, :domains])


def solution(mesh):
    placed = (
        P("dp", "mp"),
        P("dp", "mp"),
        P(),
        P(),
        P(None, ("dp", "mp")),
        P(None, ("dp", "mp")),
        P("dp"),
        P(("dp", "mp")),
        P(),
        P(),
    )
    return jax.shard_map(
        on_device,
        mesh=mesh,
        in_specs=placed,
        out_specs=(P(("dp", "mp")), P(("dp", "mp")), P(("dp", "mp")), P()),
        check_vma=False,
    )
```

```python
import functools

import jax
import jax.numpy as jnp
from jax import lax
from jax.experimental import pallas as pl
from jax.experimental.pallas import tpu as pltpu
from jax.sharding import PartitionSpec as P


AXES = ("dp", "mp")
LOW = -1e30
LANES = 128
VMEM = pl.BlockSpec(memory_space=pltpu.VMEM)
SMEM = pl.BlockSpec(memory_space=pltpu.SMEM)
HBM = pl.BlockSpec(memory_space=pltpu.HBM)


def swap(x, flip_dp, flip_mp):
    dp, mp = lax.axis_size("dp"), lax.axis_size("mp")
    pairs = [
        (d * mp + m, (d ^ flip_dp) * mp + (m ^ flip_mp)) for d in range(dp) for m in range(mp)
    ]
    return lax.ppermute(x, AXES, pairs)


def pack_kernel(count, digits, where_ref, gain_ref, *refs):
    pieces, out_ref = refs[:count], refs[-1]
    rows, depth = pieces[0].shape
    width = count * depth
    at = where_ref[1]
    total = jnp.zeros((rows, 1), jnp.float32)
    for piece in pieces:
        values = piece[...].astype(jnp.float32)
        total = total + jnp.sum(values * values, -1, keepdims=True)
    scale = lax.rsqrt(total / width + 1e-05)
    for n, piece in enumerate(pieces):
        lanes = pl.ds(pl.multiple_of((at ^ n) * depth, LANES), depth)
        values = piece[...].astype(jnp.float32)
        out_ref[:, lanes] = (values * scale * gain_ref[:, lanes]).astype(jnp.bfloat16)
    if digits:
        lane = lax.broadcasted_iota(jnp.int32, (rows, LANES), 1)
        ids = jnp.broadcast_to(refs[count][...], (rows, LANES))
        parts = jnp.where(lane < 3, jnp.right_shift(ids, 7 * jnp.minimum(lane, 3)) & 127, 0)
        out_ref[:, width:] = parts.astype(jnp.float32).astype(jnp.bfloat16)


def pack(where, gain, pieces, ids):
    rows, depth = pieces[0].shape
    width = depth * len(pieces) + (LANES if ids is not None else 0)
    extra = [] if ids is None else [ids]
    return pl.pallas_call(
        functools.partial(pack_kernel, len(pieces), ids is not None),
        in_specs=[SMEM, VMEM] + [VMEM] * (len(pieces) + len(extra)),
        out_specs=VMEM,
        out_shape=jax.ShapeDtypeStruct((rows, width), jnp.bfloat16),
        compiler_params=pltpu.CompilerParams(vmem_limit_bytes=8 * 2**20),
        name="pack",
    )(where, gain, *pieces, *extra)


def stay(x):
    return pltpu.with_memory_space_constraint(x, pltpu.HBM)


def load_kernel(plan, count, *refs):
    sources, outs, sems = refs[:count], refs[count:-1], refs[-1]
    copies = []
    for n, (at, start, size) in enumerate(plan):
        source = sources[at] if size is None else sources[at].at[pl.ds(start, size)]
        copies.append(pltpu.make_async_copy(source, outs[n], sems.at[n]))
    for copy in copies:
        copy.start()
    for copy in copies:
        copy.wait()


def load(sources, plan):
    shapes = [
        pltpu.VMEM(
            sources[at].shape if size is None else (size, sources[at].shape[1]), sources[at].dtype
        )
        for at, _, size in plan
    ]
    return pl.pallas_call(
        functools.partial(load_kernel, plan, len(sources)),
        in_specs=[HBM] * len(sources),
        out_specs=[VMEM] * len(plan),
        out_shape=shapes,
        scratch_shapes=[pltpu.SemaphoreType.DMA((len(plan),))],
        compiler_params=pltpu.CompilerParams(vmem_limit_bytes=2**20),
        name="load",
    )(*sources)


def put_in_order(x, rows, at):
    blocks = x.shape[1] // rows
    step = 1
    while step < blocks:
        other = jnp.concatenate(
            [x[:, (b ^ step) * rows : (b ^ step) * rows + rows] for b in range(blocks)], -1
        )
        x = jnp.where((at & step) != 0, other, x)
        step *= 2
    return x


def stats_kernel(chips, bounds, vocab, width, plan, mode, where_ref, *refs):
    pieces, refs = refs[:chips], refs[chips:]
    words, refs = refs[: len(bounds)], refs[len(bounds) :]
    if mode != "ref":
        ids_ref, refs = refs[0], refs[1:]
    if mode == "last":
        rm_ref, pm_ref, labels_ref, refs = *refs[:3], refs[3:]
    if plan:
        head_ref, out_ref, *outs, states, sems = refs
    else:
        out_ref, states = refs
        outs = []
    copies = [
        pltpu.make_async_copy(head_ref.at[pl.ds(*bounds[n])], outs[k], sems.at[k])
        for k, n in enumerate(plan)
    ]
    for copy in copies:
        copy.start()
    rows = pieces[0].shape[0]
    tokens = chips * rows
    for n, piece in enumerate(pieces):
        states[pl.ds(n * rows, rows), :] = piece[...]
    if mode != "ref":
        ids = ids_ref[2:3, :]
    else:
        lane = lax.broadcasted_iota(jnp.int32, (8, LANES), 1)
        digit = jnp.where(lane == 0, 1.0, jnp.where(lane == 1, 128.0, 16384.0))
        digit = jnp.where(lane < 3, digit, 0.0).astype(jnp.bfloat16)
        ids = lax.dot_general(
            digit, states[:, width:], (((1,), (1,)), ((), ())), preferred_element_type=jnp.float32
        )[0:1]
    wanted = ids.astype(jnp.int32) - where_ref[2]
    top = jnp.full((8, tokens), LOW, jnp.float32)
    total = jnp.zeros((8, tokens), jnp.float32)
    target = jnp.zeros((8, tokens), jnp.float32)
    for word, (start, size) in zip(words, bounds):
        logits = lax.dot_general(
            word[...],
            states[:, :width],
            (((1,), (1,)), ((), ())),
            preferred_element_type=jnp.float32,
        )
        row = lax.broadcasted_iota(jnp.int32, (size, tokens), 0) + start
        if start + size > vocab:
            logits = jnp.where(row < vocab, logits, LOW)
        hit = jnp.where(row == wanted, logits, 0.0)
        logits = logits.reshape(size // 8, 8, tokens)
        fresh = jnp.maximum(top, jnp.max(logits, 0))
        total = total * jnp.exp(top - fresh) + jnp.sum(jnp.exp(logits - fresh[None]), 0)
        target = target + jnp.sum(hit.reshape(size // 8, 8, tokens), 0)
        top = fresh
    peak = jnp.max(top, 0, keepdims=True)
    lse = peak + jnp.log(jnp.sum(total * jnp.exp(top - peak), 0, keepdims=True))
    target = jnp.sum(target, 0, keepdims=True)
    if mode != "last":
        out_ref[0:1, :] = lse
        out_ref[1:2, :] = target
        out_ref[2:3, :] = ids
    else:
        first = jnp.concatenate([rm_ref[0:1], pm_ref[0:1], rm_ref[1:2], pm_ref[1:2]], 0)
        second = jnp.concatenate([ids_ref[0:1], lse, ids_ref[1:2], target], 0)
        blocks = []
        for n in range(chips):
            lanes = slice(n * rows, (n + 1) * rows)
            blocks += [first[:, lanes], second[:, lanes]]
        table = put_in_order(jnp.concatenate(blocks, -1), rows, where_ref[0])
        whole = table.shape[1]
        for n in range(4):
            out_ref[:, n * whole : (n + 1) * whole] = table[n : n + 1]
        out_ref[:, 4 * whole :] = labels_ref[...]
    for copy in copies:
        copy.wait()


def stats(mode, where, words, bounds, pieces, width, vocab, head=None, plan=(), extra=()):
    chips, rows = len(pieces), pieces[0].shape[0]
    tokens = chips * rows
    shapes = [jax.ShapeDtypeStruct((3, tokens), jnp.float32)]
    if mode == "last":
        shapes = [jax.ShapeDtypeStruct((1, 10 * tokens), jnp.float32)]
    shapes += [pltpu.VMEM((bounds[n][1], width), jnp.bfloat16) for n in plan]
    scratch = [pltpu.VMEM((tokens, pieces[0].shape[1]), jnp.bfloat16)]
    args = [where, *pieces, *words, *extra]
    specs = [SMEM] + [VMEM] * (len(args) - 1)
    if plan:
        args.append(head)
        specs.append(HBM)
        scratch.append(pltpu.SemaphoreType.DMA((len(plan),)))
    return pl.pallas_call(
        functools.partial(stats_kernel, chips, bounds, vocab, width, plan, mode),
        in_specs=specs,
        out_specs=[VMEM] * len(shapes),
        out_shape=shapes,
        scratch_shapes=scratch,
        compiler_params=pltpu.CompilerParams(vmem_limit_bytes=12 * 2**20),
        cost_estimate=pl.CostEstimate(
            flops=2 * tokens * width * vocab,
            bytes_accessed=2 * width * sum(bounds[n][1] for n in plan),
            transcendentals=tokens * vocab,
        ),
        name="stats",
    )(*args)


def merge(left, right):
    peak = jnp.maximum(left, right)
    lse = peak + jnp.log(jnp.exp(left - peak) + jnp.exp(right - peak))
    lane = lax.broadcasted_iota(jnp.int32, left.shape, 1)
    return jnp.where(lane < left.shape[1] // 5 * 2, lse, left + right)


def merge_over(table, flips):
    parts = [table] + [swap(table, *flip) for flip in flips]
    step = 1
    while step < len(parts):
        parts = [
            merge(parts[n], parts[n ^ step]) if n % (2 * step) == 0 else parts[n]
            for n in range(len(parts))
        ]
        step *= 2
    return parts[0]


def finish_kernel(
    blocks, slices, buckets, domains, where_ref, table_ref, prior_ref,
    ref_ref, proxy_ref, bucket_ref, domain_ref,
):
    tokens = table_ref.shape[1] // 5
    rows = [table_ref[:, n * tokens : (n + 1) * tokens] for n in range(5)]
    ref_loss, proxy_loss = rows[0] - rows[2], rows[1] - rows[3]
    excess = jnp.maximum(proxy_loss - ref_loss, 0.0)
    label = rows[4].astype(jnp.int32)
    losses = jnp.concatenate([ref_loss, proxy_loss], 0)
    for at, count in ((where_ref[0], blocks), (where_ref[1], slices)):
        size = losses.shape[1] // count
        chosen = losses[:, :size]
        for n in range(1, count):
            chosen = jnp.where(at == n, losses[:, n * size : (n + 1) * size], chosen)
        losses = chosen
    ref_ref[...] = losses[0:1]
    proxy_ref[...] = losses[1:2]
    terms = jnp.concatenate(
        [excess, jnp.ones_like(excess), jnp.zeros((6, tokens), jnp.float32)], 0
    )

    def sums(count, first, label):
        hot = lax.broadcasted_iota(jnp.int32, (count, tokens), 0) + first == label
        part = lax.dot_general(
            terms,
            hot.astype(jnp.float32),
            (((1,), (1,)), ((), ())),
            precision=lax.Precision.HIGHEST,
            preferred_element_type=jnp.float32,
        )
        return part[0:1] / jnp.maximum(part[1:2], 1.0)

    bucket_ref[...] = sums(buckets, where_ref[3], label // domains)
    score = jnp.log(prior_ref[...]) + sums(domains, 0, label % domains)
    grown = jnp.exp(score - jnp.max(score, -1, keepdims=True))
    weights = grown / jnp.sum(grown, -1, keepdims=True)
    domain_ref[...] = jnp.log(0.999 * weights + 0.001 / domains)


def step(
    ref_hidden, proxy_hidden, ref_gain, proxy_gain, ref_head, proxy_head,
    token_ids, bucket_ids, domain_of_bucket, prior_weights,
):
    dp, mp = lax.axis_size("dp"), lax.axis_size("mp")
    dp_at, mp_at = lax.axis_index("dp"), lax.axis_index("mp")
    device = dp_at * mp + mp_at
    width = ref_hidden.shape[1] * mp
    vocab = ref_head.shape[1]
    own_rows = bucket_ids.shape[0]
    tokens = own_rows * dp * mp
    buckets, domains = domain_of_bucket.shape[0], prior_weights.shape[0]
    bucket_dev = buckets // (dp * mp)
    where = jnp.stack([dp_at, mp_at, device * vocab, device * bucket_dev]).astype(jnp.int32)

    def words_of(head):
        words = head.T
        words = jnp.pad(words, ((0, -vocab % 8), (0, 0))) if vocab % 8 else words
        return stay(words)

    ref_words, proxy_words = words_of(ref_head), words_of(proxy_head)
    height = ref_words.shape[0]
    part = height // 32 * 8
    bounds = [(n * part, part) for n in range(3)] + [(3 * part, height - 3 * part)]

    def slices(hidden):
        pieces = []
        for k in range(1, mp):
            pieces.append(swap(hidden, 0, k))
        return pieces

    def planes(states):
        mine = [states]
        for k in range(1, dp // 2):
            mine.append(swap(states, 2 * k, 0))
        theirs = []
        for piece in mine:
            theirs.append(swap(piece, 1, 0))
        return mine, theirs

    ref_slices = slices(ref_hidden)
    proxy_slices = slices(proxy_hidden)
    sources = [ref_hidden, proxy_hidden, ref_gain[None], proxy_gain[None]]
    ref_own, proxy_own, ref_scale, proxy_scale = load(
        [stay(x) for x in sources], [(n, 0, None) for n in range(4)]
    )
    ref_parts = load([ref_words], [(0, *bounds[0]), (0, *bounds[1])])
    ref_parts += load([ref_words], [(0, *bounds[2]), (0, *bounds[3])])
    ref_mine, ref_theirs = planes(
        pack(where, ref_scale, [ref_own, *ref_slices], token_ids[:, None])
    )
    proxy_mine, proxy_theirs = planes(pack(where, proxy_scale, [proxy_own, *proxy_slices], None))
    hot = bucket_ids[:, None] == lax.broadcasted_iota(jnp.int32, (1, buckets), 1)
    label = bucket_ids * domains + jnp.sum(jnp.where(hot, domain_of_bucket[None], 0), -1)
    labels = lax.dynamic_update_slice(
        jnp.zeros((1, tokens), jnp.float32),
        label.astype(jnp.float32)[None],
        (0, device * own_rows),
    )
    ref_first, *parts = stats(
        "ref", where, ref_parts, bounds, ref_mine, width, vocab, proxy_words, (0, 1)
    )
    ref_second, *others = stats(
        "ref", where, ref_parts, bounds, ref_theirs, width, vocab, proxy_words, (2, 3)
    )
    parts += others
    (proxy_first,) = stats(
        "proxy", where, parts, bounds, proxy_mine, width, vocab, extra=(ref_first,)
    )
    (table,) = stats(
        "last", where, parts, bounds, proxy_theirs, width, vocab,
        extra=(ref_second, ref_first, proxy_first, labels),
    )
    table = merge_over(table, [(1, 0)])
    table = merge_over(table, [(2 * k, 0) for k in range(1, dp // 2)])
    table = merge_over(table, [(0, k) for k in range(1, mp)])

    ref_loss, proxy_loss, bucket_excess, domain_log_weights = pl.pallas_call(
        functools.partial(finish_kernel, dp, mp, bucket_dev, domains),
        in_specs=[SMEM, VMEM, VMEM],
        out_specs=[VMEM] * 4,
        out_shape=[
            jax.ShapeDtypeStruct((1, own_rows), jnp.float32),
            jax.ShapeDtypeStruct((1, own_rows), jnp.float32),
            jax.ShapeDtypeStruct((1, bucket_dev), jnp.float32),
            jax.ShapeDtypeStruct((1, domains), jnp.float32),
        ],
        name="finish",
    )(where, table, prior_weights[None])
    return (ref_loss[0], proxy_loss[0], bucket_excess[0], domain_log_weights[0])


def solution(mesh):
    placed = (
        P("dp", "mp"),
        P("dp", "mp"),
        P(),
        P(),
        P(None, ("dp", "mp")),
        P(None, ("dp", "mp")),
        P("dp"),
        P(("dp", "mp")),
        P(),
        P(),
    )
    return jax.shard_map(
        step,
        mesh=mesh,
        in_specs=placed,
        out_specs=(P(("dp", "mp")), P(("dp", "mp")), P(("dp", "mp")), P()),
        check_vma=False,
    )
```
